32 devices in a mesh: dp: 4 (over x, core), graph: 8 (over z, y).
Axes of the slice: x: 2, y: 2, z: 4, core: 2. Of those that a mesh axis runs over, the one named last changes fastest.
Arguments:
- atoms: bfloat16 [4, 512, 256], P('dp', 'graph'), may hold values from -6 to 6
- grad_out: bfloat16 [4, 512, 256], P('dp', 'graph'), may hold values from -6 to 6
- w_edge: bfloat16 [640, 1024], P('dp'), may hold values from -0.25 to 0.25
- w_down: bfloat16 [1024, 256], P('dp'), may hold values from -0.1875 to 0.1875
- w_up: bfloat16 [256, 1024], P('dp'), may hold values from -0.375 to 0.375
- w_out: bfloat16 [1024, 256], P('dp'), may hold values from -0.1875 to 0.1875
- w_sbf: bfloat16 [42, 256], P(None, 'dp'), may hold values from -1 to 1
- send_list: int32 [4, 8, 32], P('dp', 'graph'), may hold values from 0 to 63
- edge_src: int32 [4, 8, 1024], P('dp', 'graph'), may hold values from 0 to 95
- edge_tgt: int32 [4, 8, 1024], P('dp', 'graph'), may hold values from 0 to 63
- edge_count: int32 [4, 8], P('dp', 'graph'), may hold values from 256 to 1024, as said below
- radial: bfloat16 [4, 8, 1024, 128], P('dp', 'graph'), may hold values from -6 to 6
- angular: bfloat16 [4, 8, 42, 2048], P('dp', 'graph'), may hold values from -6 to 6
- trip_from: int32 [4, 8, 2048], P('dp', 'graph'), may hold values from 0 to 1023, as said below
- trip_into: int32 [4, 8, 2048], P('dp', 'graph'), may hold values from 0 to 1023, as said below
Outputs:
- atoms_out: bfloat16 [4, 512, 256], P('dp', 'graph')
- atoms_grad: float32 [4, 512, 256], P('dp', 'graph')
- edge_grad: float32 [640, 1024], P('dp')
- down_grad: float32 [1024, 256], P('dp')
- up_grad: float32 [256, 1024], P('dp')
- out_grad: float32 [1024, 256], P('dp')
- sbf_grad: float32 [42, 256], P(None, 'dp')
The draws below stay inside these ranges and needn't reach their ends.
Inputs may be any that keep to these rules, and one draw needn't show every extreme that they name: `edge_count`: in every snapshot some piece has all 1024 slots live. `trip_from`: each index is below the live edge count of its piece. `trip_into`: each index is below the live edge count of its piece.
All inputs are finite; a program needn't handle non-finite values.
Results may differ from the reference program's by a relative error of at most 0.024.
Values may be sent and summed in bfloat16 or wider, within the bound.
No kernel may reach another device: no remote copies, remote signals or barrier semaphores. Data moves between devices by JAX's collectives and lax.ppermute only.
A program may use at most 64 MiB of HBM per device.

```python
import jax
import jax.numpy as jnp
from jax import lax

HA = 256
EW = 1024
TW = 256
RBF = 128
SBF_K = 42
A_DEV = 64
E_DEV = 1024
TRIP_DEV = 2048
GS = 4
SNAPS = 4
SHARDS = 8
ATOMS = 512
EDGE_IN = 640


def edge_counts(key):
    base = jax.random.randint(jax.random.fold_in(key, 11), (SNAPS, SHARDS), E_DEV // 4, E_DEV + 1)
    busiest = jax.random.randint(jax.random.fold_in(key, 12), (SNAPS, 1), 0, SHARDS)
    return jnp.where(jnp.arange(SHARDS)[None, :] == busiest, E_DEV, base).astype(jnp.int32)


def draw_edge_count(key, part):
    return edge_counts(key)


def draw_trip_from(key, part):
    counts = edge_counts(key)
    return jax.random.randint(jax.random.fold_in(key, 21), (SNAPS, SHARDS, TRIP_DEV), 0, counts[:, :, None]).astype(jnp.int32)


def draw_trip_into(key, part):
    counts = edge_counts(key)
    return jax.random.randint(jax.random.fold_in(key, 22), (SNAPS, SHARDS, TRIP_DEV), 0, counts[:, :, None]).astype(jnp.int32)


def touch_ends(array, key, least, high):
    longest = array.shape.index(max(array.shape))
    spots = []
    for shift in (0, 1):
        where = [jax.random.randint(jax.random.fold_in(key, axis), (), 0, length) for axis, length in enumerate(array.shape)]
        where[longest] = (where[longest] + shift) % array.shape[longest]
        spots.append(tuple(where))
    return array.at[spots[0]].set(least).at[spots[1]].set(high)


def block_levels(own_key, shape, shards, smallest, high):
    def one(position, blocks):
        heights = jax.random.uniform(jax.random.fold_in(jax.random.fold_in(own_key, 6), position), (blocks,), jnp.float32, smallest / len(shards), high / len(shards))
        return jnp.repeat(jnp.exp(heights), shape[position] // blocks).reshape((-1,) + (1,) * (len(shape) - position - 1))

    level = one(*shards[0])
    for cut in shards[1:]:
        level = level * one(*cut)
    return level


def normal_values(key, shape, deviation, most, split=(), kind=jnp.bfloat16):
    gain = block_levels(key, shape, split, -0.22, 0.18) if split else 1.0
    values = jax.random.normal(key, shape, jnp.float32) * deviation * gain
    return jnp.minimum(jnp.maximum(values, -most), most).astype(kind)


def setup_inputs(seed: int = 0) -> dict:
    seeds = jax.random.split(jax.random.key(seed), 16)
    return {
        "atoms": normal_values(seeds[0], (SNAPS, ATOMS, HA), 1.0, 6.0, ((0, 4), (1, 8))),
        "grad_out": normal_values(seeds[1], (SNAPS, ATOMS, HA), 1.0, 6.0, ((0, 4), (1, 8))),
        "w_edge": normal_values(seeds[2], (EDGE_IN, EW), EDGE_IN ** -0.5, 0.25, ((0, 4),)),
        "w_down": normal_values(seeds[3], (EW, TW), EW ** -0.5, 0.1875, ((0, 4),)),
        "w_up": normal_values(seeds[4], (TW, EW), TW ** -0.5, 0.375, ((0, 4),)),
        "w_out": normal_values(seeds[5], (EW, HA), EW ** -0.5, 0.1875, ((0, 4),)),
        "w_sbf": normal_values(seeds[6], (SBF_K, TW), SBF_K ** -0.5, 1.0, ((1, 4),)),
        "send_list": touch_ends(jax.random.randint(seeds[7], (SNAPS, SHARDS, SHARDS * GS), 0, A_DEV), jax.random.fold_in(seeds[7], 1), 0, A_DEV - 1).astype(jnp.int32),
        "edge_src": touch_ends(jax.random.randint(seeds[8], (SNAPS, SHARDS, E_DEV), 0, A_DEV + SHARDS * GS), jax.random.fold_in(seeds[8], 1), 0, (A_DEV + SHARDS * GS) - 1).astype(jnp.int32),
        "edge_tgt": touch_ends(jax.random.randint(seeds[9], (SNAPS, SHARDS, E_DEV), 0, A_DEV), jax.random.fold_in(seeds[9], 1), 0, A_DEV - 1).astype(jnp.int32),
        "edge_count": draw_edge_count(jax.random.fold_in(seeds[15], 71), 0),
        "radial": normal_values(seeds[11], (SNAPS, SHARDS, E_DEV, RBF), 1.0, 6.0, ((0, 4), (1, 8))),
        "angular": normal_values(seeds[12], (SNAPS, SHARDS, SBF_K, TRIP_DEV), 1.0, 6.0, ((0, 4), (1, 8))),
        "trip_from": draw_trip_from(jax.random.fold_in(seeds[15], 71), 0),
        "trip_into": draw_trip_into(jax.random.fold_in(seeds[15], 71), 0),
    }


def edge_block(atom_rows, ghost_rows, weights, source, target, live, radial_rows, angular_rows, trip_first, trip_second):
    w_edge, w_down, w_up, w_out, w_sbf = weights
    extended = jnp.concatenate([atom_rows, ghost_rows], axis=0)
    features = jnp.concatenate([extended[source], atom_rows[target], radial_rows], axis=1)
    preact = jnp.dot(features, w_edge, preferred_element_type=jnp.float32)
    message = (jax.nn.silu(preact) * live[:, None]).astype(jnp.bfloat16)
    message = lax.optimization_barrier(message)
    reduced = jnp.dot(message, w_down, preferred_element_type=jnp.float32).astype(jnp.bfloat16)
    basis = jnp.dot(angular_rows.T, w_sbf, preferred_element_type=jnp.float32)
    triple = reduced[trip_first].astype(jnp.float32) * basis
    summed = jax.ops.segment_sum(triple, trip_second, num_segments=reduced.shape[0]).astype(jnp.bfloat16)
    raised = jnp.dot(summed, w_up, preferred_element_type=jnp.float32)
    merged = (message.astype(jnp.float32) + raised).astype(jnp.bfloat16)
    projected = jnp.dot(merged, w_out, preferred_element_type=jnp.float32)
    update = jax.ops.segment_sum(projected, target, num_segments=atom_rows.shape[0])
    return atom_rows.astype(jnp.float32) + update

def pick_rows(table_rows, chosen):
    return table_rows[chosen]

def spread_rows(values, chosen):
    return jax.ops.segment_sum(values.astype(jnp.float32), chosen, num_segments=A_DEV)

def reference(atoms, grad_out, w_edge, w_down, w_up, w_out, w_sbf, send_list, edge_src, edge_tgt, edge_count, radial, angular, trip_from, trip_into):
    pieces = SNAPS * SHARDS
    atom_blocks = atoms.reshape(SNAPS, SHARDS, A_DEV, HA)
    picked = jax.vmap(jax.vmap(pick_rows))(atom_blocks, send_list)
    ghosts = picked.reshape(SNAPS, SHARDS, SHARDS, GS, HA).transpose(0, 2, 1, 3, 4).reshape(pieces, SHARDS * GS, HA)
    live = (jnp.arange(E_DEV, dtype=jnp.int32)[None, :] < edge_count.reshape(pieces, 1)).astype(jnp.float32)
    weights = (w_edge, w_down, w_up, w_out, w_sbf)
    zeros = tuple((jnp.zeros(weight.shape, jnp.float32) for weight in weights))

    def one_piece(totals, inputs):
        atom_rows, ghost_rows, upstream, source, target, live_row, radial_rows, angular_rows, trip_first, trip_second = inputs

        def local(rows_in, ghosts_in, params):
            return edge_block(rows_in, ghosts_in, params, source, target, live_row, radial_rows, angular_rows, trip_first, trip_second)
        value, pull = jax.vjp(local, atom_rows, ghost_rows, weights)
        d_rows, d_ghosts, d_params = pull(upstream.astype(jnp.float32))
        totals = jax.tree.map(lambda running, term: running + term.astype(jnp.float32), totals, d_params)
        return (totals, (value.astype(jnp.bfloat16), d_rows, d_ghosts))
    inputs = (atom_blocks.reshape(pieces, A_DEV, HA), ghosts, grad_out.reshape(pieces, A_DEV, HA), edge_src.reshape(pieces, E_DEV), edge_tgt.reshape(pieces, E_DEV), live, radial.reshape(pieces, E_DEV, RBF), angular.reshape(pieces, SBF_K, TRIP_DEV), trip_from.reshape(pieces, TRIP_DEV), trip_into.reshape(pieces, TRIP_DEV))
    totals, (outputs, d_rows, d_ghosts) = lax.scan(one_piece, zeros, inputs)
    returned = d_ghosts.reshape(SNAPS, SHARDS, SHARDS, GS, HA).transpose(0, 2, 1, 3, 4).reshape(pieces, SHARDS * GS, HA)
    added = jax.vmap(spread_rows)(returned, send_list.reshape(pieces, SHARDS * GS))
    atoms_grad = (d_rows.astype(jnp.float32) + added).reshape(SNAPS, ATOMS, HA)
    atoms_out = outputs.reshape(SNAPS, ATOMS, HA)
    return (atoms_out, atoms_grad, totals[0], totals[1], totals[2], totals[3], totals[4])
```

```python
import functools

import jax
import jax.numpy as jnp
from jax import lax
from jax.experimental import pallas as pl
from jax.experimental.pallas import tpu as pltpu
from jax.sharding import PartitionSpec as P

F32 = jnp.float32
BF16 = jnp.bfloat16
PARTS = 4
VM = pl.BlockSpec(memory_space=pltpu.VMEM)
SM = pl.BlockSpec(memory_space=pltpu.SMEM)


def nn(a, b):
    return jnp.dot(a, b, preferred_element_type=F32)


def nt(a, b):
    return lax.dot_general(a, b, (((1,), (1,)), ((), ())), preferred_element_type=F32)


def rows_iota(shape):
    return lax.broadcasted_iota(jnp.int32, shape, 0)


def assemble(dst, shards, me):
    size = shards[0].shape[0]
    for rel, shard in enumerate(shards):
        at = pl.multiple_of((me ^ rel) * size, size)
        dst[pl.ds(at, size), :] = shard[...]


def reversed_bits(value, bits):
    out = 0
    for bit in range(bits):
        out |= ((value >> bit) & 1) << (bits - 1 - bit)
    return out


def prepare_body(info, src, tgt, into, radial, st_ref, f_ref, rad_ref, sc_ref, *, atoms, ghosts):
    count = info[2]
    slots = src.shape[1]
    width = f_ref.shape[1]
    used = st_ref.shape[0] - radial.shape[1]
    live = lax.broadcasted_iota(jnp.int32, (1, slots), 1) < count
    first = jnp.where(live, src[...], -1)
    second = jnp.where(live, tgt[...] + (atoms + ghosts), -1)
    step = 256
    for at in range(0, slots, step):
        grid = rows_iota((width, step))
        hot = (grid == first[:, at : at + step]) | (grid == second[:, at : at + step])
        hot = hot.astype(F32)
        st_ref[:used, at : at + step] = hot[:used].astype(BF16)
        f_ref[at : at + step, :] = hot.T.astype(BF16)
        keep = (rows_iota((step, radial.shape[1])) + at) < count
        rows = jnp.where(keep, radial[at : at + step, :].astype(F32), 0.0)
        rad_ref[at : at + step, :] = rows.astype(BF16)
        st_ref[used:, at : at + step] = rows.T.astype(BF16)
    owner = (rows_iota((atoms, slots)) == tgt[...]).astype(F32).astype(BF16)
    trips = into.shape[1]
    for at in range(0, trips, 512):
        hot = (rows_iota((slots, 512)) == into[:, at : at + 512]).astype(F32).astype(BF16)
        sc_ref[:, at : at + 512] = nn(owner, hot).astype(BF16)


def early_body(*refs, nd):
    info, gout, angular, source, sc = refs[:5]
    wo, wu, ws = refs[5 : 5 + nd], refs[5 + nd : 5 + 2 * nd], refs[5 + 2 * nd : 5 + 3 * nd]
    go_ref, gu_ref, dr_ref, drt_ref = refs[5 + 3 * nd : 9 + 3 * nd]
    wo_s, wu_s, ws_s, drf_s = refs[9 + 3 * nd :]
    me = info[0]
    assemble(wo_s, wo, me)
    assemble(wu_s, wu, me)
    assemble(ws_s, ws, me)
    go = nt(gout[...], wo_s[...]).astype(BF16)
    go_ref[...] = go
    gu = nt(wu_s[...], go).astype(BF16)
    gu_ref[...] = gu
    trips = source.shape[1]
    for at in range(0, trips, 512):
        basis = nn(ws_s[...], angular[:, at : at + 512])
        back = nn(gu, sc[:, at : at + 512])
        drf_s[:, at : at + 512] = (basis * back).astype(BF16)
    slots = dr_ref.shape[0]

    def block(i, carry):
        at = pl.multiple_of(i * 256, 256)
        hot = ((rows_iota((256, trips)) + at) == source[...]).astype(F32).astype(BF16)
        rows = nt(hot, drf_s[...])
        dr_ref[pl.ds(at, 256), :] = rows.astype(BF16)
        drt_ref[:, pl.ds(at, 256)] = rows.T.astype(BF16)
        return carry

    lax.fori_loop(0, slots // 256, block, 0)


def edge_body(*refs, nd, atoms, ghosts):
    info, st, fm, rad, atm, gho, gout, go, dr, drt = refs[:10]
    we, wd = refs[10 : 10 + nd], refs[10 + nd : 10 + 2 * nd]
    msg_ref, datm_ref, dgho_ref, keep_ref, send_ref = refs[10 + 2 * nd : 15 + 2 * nd]
    we_s, wd_s, ext_s, p_s, g_s, dp_s, eg_s, dg_s, dx_s = refs[15 + 2 * nd :]
    me, own = info[0], info[1]
    slots = fm.shape[0]
    used = ext_s.shape[0]
    ha = atm.shape[1]
    ext = atoms + ghosts
    lanes = keep_ref.shape[3]
    assemble(we_s, we, me)
    assemble(wd_s, wd, me)
    ext_s[:atoms, :] = atm[...]
    ext_s[atoms:ext, :] = gho[...]
    ext_s[ext:, :] = atm[...]
    g_s[...] = jnp.zeros_like(g_s)
    p_s[...] = jnp.zeros_like(p_s)
    dx_s[...] = jnp.zeros_like(dx_s)
    turned = ext_s[...].astype(F32).T.astype(BF16)
    tall = 256

    def column(cb, carry):
        at = pl.multiple_of(cb * 256, 256)
        cols = pl.ds(at, 256)
        p_s[:ext, :] = nn(ext_s[:ext, :], we_s[:ha, cols]).astype(BF16)
        p_s[ext:used, :] = nn(ext_s[ext:, :], we_s[ha : 2 * ha, cols]).astype(BF16)
        g_s[ext:used, :] = go[:, cols]
        down = wd_s[pl.ds(at, 256), :]
        table = p_s[...]
        upper = g_s[...]
        wrad = we_s[2 * ha :, cols]
        for rb in range(0, slots, tall):
            hot = fm[rb : rb + tall, :]
            x = nn(hot, table) + nn(rad[rb : rb + tall, :], wrad)
            sig = 0.5 * jnp.tanh(0.5 * x) + 0.5
            out = x * sig
            msg_ref[cb, rb : rb + tall, :] = out.astype(BF16)
            dm = nn(hot, upper) + nt(dr[rb : rb + tall, :], down)
            dp_s[rb : rb + tall, :] = (dm * (sig + out * (1.0 - sig))).astype(BF16)
        u = nn(st[...], dp_s[...])
        ub = u.astype(BF16)
        eg_s[:ha, :] = nn(turned[:, :ext], ub[:ext]).astype(BF16)
        eg_s[ha : 2 * ha, :] = nn(turned[:, ext:], ub[ext:used]).astype(BF16)
        eg_s[2 * ha :, :] = ub[used:]
        dx_s[:ext, :] += nt(ub[:ext], we_s[:ha, cols])
        dx_s[ext:, :] += nt(ub[ext:used], we_s[ha : 2 * ha, cols])
        dg_s[cb] = nn(drt[...], msg_ref[cb]).astype(BF16)
        place = cb ^ own
        size = eg_s.shape[0] // nd
        for rel in range(nd):
            j = reversed_bits(rel, nd.bit_length() - 1)
            ref = keep_ref if j < nd // 2 else send_ref
            j = j % (nd // 2)
            row = pl.multiple_of((me ^ rel) * size, size)
            for q in range(256 // lanes):
                ref[j, place, q * size : (q + 1) * size, :] = eg_s[pl.ds(row, size), q * lanes : (q + 1) * lanes]
        return carry

    lax.fori_loop(0, PARTS, column, 0)
    grad = dx_s[:atoms, :] + dx_s[ext:, :] + gout[...].astype(F32)
    datm_ref[...] = grad
    dgho_ref[...] = dx_s[atoms:ext, :].astype(BF16)
    size = eg_s.shape[0] // nd * (256 // lanes)
    place_columns(dg_s, keep_ref, send_ref, me, own, nd, lanes, size)


def place_columns(table, keep_ref, send_ref, me, own, nd, lanes, row):
    per = 256 // lanes
    tall = table.shape[1] // PARTS
    for rel in range(nd):
        j = reversed_bits(rel, nd.bit_length() - 1)
        ref = keep_ref if j < nd // 2 else send_ref
        j = j % (nd // 2)
        shard = me ^ rel
        for b in range(PARTS):
            block = table[shard // per, b * tall : (b + 1) * tall, :]
            value = block[:, :lanes]
            for q in range(1, per):
                value = jnp.where(shard % per == q, block[:, q * lanes : (q + 1) * lanes], value)
            ref[j, b ^ own, row : row + tall, :] = value


def late_body(*refs, nd, atoms, ghosts):
    info, msg, st, sc, source, angular, go, gu, gout, atm = refs[:10]
    wd, wo = refs[10 : 10 + nd], refs[10 + nd : 10 + 2 * nd]
    wu, ws = refs[10 + 2 * nd : 10 + 3 * nd], refs[10 + 3 * nd : 10 + 4 * nd]
    out_ref, keep_ref, send_ref = refs[10 + 4 * nd : 13 + 4 * nd]
    wd_s, wo_s, wu_s, ws_s, red_s, tri_s, db_s, mt_s, og_s, ug_s, sg_s = refs[13 + 4 * nd :]
    me, own = info[0], info[1]
    ext = atoms + ghosts
    slots = msg.shape[1]
    trips = source.shape[1]
    lanes = keep_ref.shape[3]
    assemble(wd_s, wd, me)
    assemble(wo_s, wo, me)
    assemble(wu_s, wu, me)
    assemble(ws_s, ws, me)
    for rb in range(0, slots, 256):
        rows = nn(msg[0, rb : rb + 256, :], wd_s[:256, :])
        for cb in range(1, PARTS):
            rows += nn(msg[cb, rb : rb + 256, :], wd_s[cb * 256 : (cb + 1) * 256, :])
        red_s[:, rb : rb + 256] = rows.T.astype(BF16)

    def chunk(i, carry):
        cols = pl.ds(pl.multiple_of(i * 256, 256), 256)
        hot = (rows_iota((slots, 256)) == source[:, cols]).astype(F32).astype(BF16)
        taken = nn(red_s[...], hot)
        basis = nn(ws_s[...], angular[:, cols])
        back = nn(gu[...], sc[:, cols])
        tri_s[:, cols] = (taken * basis).astype(BF16)
        db_s[:, cols] = (taken * back).astype(BF16)
        return carry

    lax.fori_loop(0, trips // 256, chunk, 0)
    held = nt(sc[...], tri_s[...]).astype(BF16)
    turned = nt(tri_s[...], sc[...]).astype(BF16)
    sg_s[:, : angular.shape[0]] = nt(db_s[...], angular[...])
    gturn = gout[...].astype(F32).T.astype(BF16)
    pick = st[ext : ext + atoms, :]
    for cb in range(PARTS):
        cols = slice(cb * 256, (cb + 1) * 256)
        total = nn(pick, msg[cb]) + nn(held, wu_s[:, cols])
        mt = total.astype(BF16)
        mt_s[:, cols] = mt
        og_s[cb] = nn(gturn, mt).astype(BF16)
        ug_s[cb] = nn(turned, go[:, cols]).astype(BF16)
    update = nn(mt_s[...], wo_s[...])
    out_ref[...] = (atm[...].astype(F32) + update).astype(BF16)
    place_columns(og_s, keep_ref, send_ref, me, own, nd, lanes, 0)
    size = ug_s.shape[1] // nd
    base = og_s.shape[1] // PARTS
    small = sg_s.shape[0] // nd // PARTS
    last = base + size * (256 // lanes)
    for rel in range(nd):
        j = reversed_bits(rel, nd.bit_length() - 1)
        ref = keep_ref if j < nd // 2 else send_ref
        j = j % (nd // 2)
        row = pl.multiple_of((me ^ rel) * size, size)
        for b in range(PARTS):
            for q in range(256 // lanes):
                ref[j, b ^ own, base + q * size : base + (q + 1) * size, :] = ug_s[
                    b, pl.ds(row, size), q * lanes : (q + 1) * lanes
                ]
            at = pl.multiple_of((me ^ rel) * small * PARTS + small * b, small)
            piece = sg_s[pl.ds(at, small), :]
            if small < 16:
                piece = jnp.concatenate([piece, jnp.zeros((16 - small, 128), F32)], axis=0)
            ref[j, b ^ own, last : last + 16, :128] = piece.astype(BF16)


def finish_body(*refs, nd):
    info, senders, back, datm = refs[:4]
    eb, rb = refs[4:8], refs[8:12]
    ag_ref, e_ref, d_ref, u_ref, o_ref, s_ref = refs[12:18]
    ebs, rbs = refs[18:]
    own = info[1]
    for p in range(PARTS):
        ebs[p] = eb[p][0]
        rbs[p] = rb[p][0]
    atoms = datm.shape[0]
    hot = (rows_iota((atoms, senders.shape[1])) == senders[...]).astype(F32).astype(BF16)
    ag_ref[...] = datm[...] + nn(hot, back[...])
    lanes = ebs.shape[2]
    rows = e_ref.shape[0]
    per = 256 // lanes
    downs, outs, smalls = [], [], []
    ups = u_ref.shape[0]
    small = s_ref.shape[1] // PARTS
    for b in range(PARTS):
        p = b ^ own
        for q in range(per):
            at = b * 256 + q * lanes
            e_ref[:, at : at + lanes] = ebs[p, q * rows : (q + 1) * rows, :].astype(F32)
            u_ref[:, at : at + lanes] = rbs[p, 64 + q * ups : 64 + (q + 1) * ups, :].astype(F32)
        downs.append(ebs[p, rows * per : rows * per + 64, :].astype(F32))
        outs.append(rbs[p, :64, :].astype(F32))
        last = 64 + ups * per
        smalls.append(rbs[p, last : last + 16, :128].astype(F32)[:small])
    d_ref[...] = jnp.concatenate(downs, axis=0).T
    o_ref[...] = jnp.concatenate(outs, axis=0).T
    table = jnp.concatenate(smalls, axis=0)
    s_ref[...] = table.T[: s_ref.shape[0], :]


def call(body, outs, scratch=()):
    def run(scalars, *arrays):
        return pl.pallas_call(
            body,
            in_specs=[SM] + [VM] * len(arrays),
            out_specs=[VM] * len(outs),
            out_shape=[jax.ShapeDtypeStruct(s, t) for s, t in outs],
            scratch_shapes=[pltpu.VMEM(s, t) for s, t in scratch],
        )(scalars, *arrays)

    return run


def swap(value, axis, size, bit):
    return lax.ppermute(value, axis, [(i, i ^ bit) for i in range(size)])


def gathered(shard, size):
    held = {0: shard}
    bit = size // 2
    while bit:
        for rel in list(held):
            held[rel | bit] = swap(held[rel], "dp", size, bit)
        bit //= 2
    return [held[rel] for rel in range(size)]


def total(keep, send, nd, ng):
    bit = 1
    while bit < nd:
        got = swap(send, "dp", nd, bit)
        half = keep.shape[0] // 2
        if half:
            send = keep[half:] + got[half:]
            keep = keep[:half] + got[:half]
        else:
            send = keep[0, 2:] + got[0, 2:]
            keep = keep[0, :2] + got[0, :2]
        bit *= 2
    got = swap(send, "graph", ng, 1)
    send = keep[1:] + got[1:]
    keep = keep[:1] + got[:1]
    keep = keep + swap(send, "graph", ng, 2)
    bit = 4
    while bit < ng:
        keep = keep + swap(keep, "graph", ng, bit)
        bit *= 2
    one = swap(keep, "graph", ng, 2)
    two = swap(keep, "graph", ng, 1)
    three = swap(one, "graph", ng, 1)
    return [keep, one, two, three]


def shards(
    atoms,
    grad_out,
    w_edge,
    w_down,
    w_up,
    w_out,
    w_sbf,
    send_list,
    edge_src,
    edge_tgt,
    edge_count,
    radial,
    angular,
    trip_from,
    trip_into,
    nd,
    ng,
):
    atm, gout = atoms[0], grad_out[0]
    na, ha = atm.shape
    senders = send_list[0, 0]
    nghost = senders.shape[0]
    ext = na + nghost
    used = ext + na
    width = -(-used // 128) * 128
    slots = edge_src.shape[2]
    trips = trip_from.shape[2]
    ew = w_edge.shape[1]
    ein = w_edge.shape[0] * nd
    tw = w_down.shape[1]
    rbf = radial.shape[3]
    sbf = w_sbf.shape[0]
    lanes = ew // nd
    me = lax.axis_index("dp")
    graph = lax.axis_index("graph")
    own = (graph & 1) * 2 + ((graph >> 1) & 1)
    info = jnp.stack([me, own, edge_count[0, 0]]).astype(jnp.int32)

    wo = gathered(w_out, nd)
    wu = gathered(w_up, nd)
    ws = gathered(w_sbf.T, nd)
    wd = gathered(w_down, nd)
    we = gathered(w_edge, nd)
    ghost = lax.all_to_all(atm[senders], "graph", split_axis=0, concat_axis=0, tiled=True)

    st, fm, rad, sc = call(
        functools.partial(prepare_body, atoms=na, ghosts=nghost),
        [((used + rbf, slots), BF16), ((slots, width), BF16), ((slots, rbf), BF16), ((na, trips), BF16)],
    )(info, edge_src[0], edge_tgt[0], trip_into[0], radial[0, 0])

    go, gu, dr, drt = call(
        functools.partial(early_body, nd=nd),
        [((na, ew), BF16), ((tw, na), BF16), ((slots, tw), BF16), ((tw, slots), BF16)],
        [((ew, ha), BF16), ((tw, ew), BF16), ((tw, sbf), BF16), ((tw, trips), BF16)],
    )(info, gout, angular[0, 0], trip_from[0], sc, *wo, *wu, *ws)

    erows = ein // nd * (256 // lanes) + tw // PARTS
    msg, datm, dgho, ekeep, esend = call(
        functools.partial(edge_body, nd=nd, atoms=na, ghosts=nghost),
        [
            ((PARTS, slots, ew // PARTS), BF16),
            ((na, ha), F32),
            ((nghost, ha), BF16),
            ((nd // 2, PARTS, erows, lanes), BF16),
            ((nd // 2, PARTS, erows, lanes), BF16),
        ],
        [
            ((ein, ew), BF16),
            ((ew, tw), BF16),
            ((used, ha), BF16),
            ((width, 256), BF16),
            ((width, 256), BF16),
            ((slots, 256), BF16),
            ((ein, 256), BF16),
            ((PARTS, tw, 256), BF16),
            ((used, ha), F32),
        ],
    )(info, st, fm, rad, atm, ghost, gout, go, dr, drt, *we, *wd)

    back = lax.all_to_all(dgho, "graph", split_axis=0, concat_axis=0, tiled=True)
    rrows = ha // PARTS + tw // nd * (256 // lanes) + 16
    value, rkeep, rsend = call(
        functools.partial(late_body, nd=nd, atoms=na, ghosts=nghost),
        [
            ((na, ha), BF16),
            ((nd // 2, PARTS, rrows, lanes), BF16),
            ((nd // 2, PARTS, rrows, lanes), BF16),
        ],
        [
            ((ew, tw), BF16),
            ((ew, ha), BF16),
            ((tw, ew), BF16),
            ((tw, sbf), BF16),
            ((tw, slots), BF16),
            ((tw, trips), BF16),
            ((tw, trips), BF16),
            ((na, ew), BF16),
            ((PARTS, ha, 256), BF16),
            ((PARTS, tw, 256), BF16),
            ((tw, 128), F32),
        ],
    )(info, msg, st, sc, trip_from[0], angular[0, 0], go, gu, gout, atm, *wd, *wo, *wu, *ws)

    eblocks = total(ekeep, esend, nd, ng)
    rblocks = total(rkeep, rsend, nd, ng)
    agrad, egrad, dgrad, ugrad, ograd, sgrad = call(
        functools.partial(finish_body, nd=nd),
        [
            ((na, ha), F32),
            ((ein // nd, ew), F32),
            ((ew // nd, tw), F32),
            ((tw // nd, ew), F32),
            ((ew // nd, ha), F32),
            ((sbf, tw // nd), F32),
        ],
        [((PARTS, erows, lanes), BF16), ((PARTS, rrows, lanes), BF16)],
    )(info, send_list[0], back, datm, *eblocks, *rblocks)
    return value[None], agrad[None], egrad, dgrad, ugrad, ograd, sgrad


def solution(mesh):
    nd, ng = mesh.shape["dp"], mesh.shape["graph"]
    three, four, split = P("dp", "graph", None), P("dp", "graph", None, None), P("dp", None)
    in_specs = (
        (three, three, split, split, split, split, P(None, "dp"), three, three, three)
        + (P("dp", "graph"), four, four, three, three)
    )
    out_specs = (three, three, split, split, split, split, P(None, "dp"))
    body = functools.partial(shards, nd=nd, ng=ng)
    return jax.shard_map(body, mesh=mesh, in_specs=in_specs, out_specs=out_specs, check_vma=False)
```
